256 devices in a mesh: gx: 8 (over x, core), gy: 8 (over z_lo, y), gz: 4 (over z_hi).
Axes of the slice: x: 4, y: 4, z: 8 (z_hi: 4, z_lo: 2; z = z_hi * 2 + z_lo), core: 2. Of those that a mesh axis runs over, the one named last changes fastest.
Arguments:
- bead_pos: float32 [3, 16, 32, 8, 128], P(None, 'gx', 'gy', 'gz'), may hold values from 0 to 3
- bead_vel: float32 [3, 16, 32, 8, 128], P(None, 'gx', 'gy', 'gz'), may hold values from -6 to 6
- bead_force: float32 [3, 16, 32, 8, 128], P(None, 'gx', 'gy', 'gz'), may hold values from -60 to 60
- cell_count: int32 [16, 32, 8], P('gx', 'gy', 'gz'), may hold values from 0 to 128
- pair_seed: int32 [16, 32, 8, 128], P('gx', 'gy', 'gz'), may hold values from 0 to 4095
- bead_half: int32 [16, 32, 8, 128], P('gx', 'gy', 'gz'), may hold values from 0 to 1
- grid_vel: float32 [3, 16, 32, 16], P(None, 'gx', ('gy', 'gz')), may hold values from -6 to 6
- correlation_map: int32 [16, 32, 16], P('gx', ('gy', 'gz')), may hold values 0 or 1
Outputs:
- new_positions: float32 [3, 16, 32, 8, 128], P(None, 'gx', 'gy', 'gz')
- new_velocities: float32 [3, 16, 32, 8, 128], P(None, 'gx', 'gy', 'gz')
- grid_velocity: float32 [3, 16, 32, 16], P(None, 'gx', ('gy', 'gz'))
- pressure: float32 [16, 32, 16], P('gx', ('gy', 'gz'))
- brick_velocity: float32 [3, 16, 32, 16], P(None, 'gx', 'gy', 'gz')
The draws below stay inside these ranges and needn't reach their ends.
Inputs may be any that keep to these rules, and one draw needn't show every extreme that they name: `cell_count`: slots below a cell's count hold beads, the others are padding.
All inputs are finite; a program needn't handle non-finite values. No bound on the sum of `correlation_map` on one device may be relied on, other than what follows from the above.
Results may differ from the reference program's by a relative error of at most 0.0003.
Values sent between devices are 32-bit elements; how exact they have to be, the bound alone decides.
No kernel may reach another device: no remote copies, remote signals or barrier semaphores. Data moves between devices by JAX's collectives and lax.ppermute only.
A program may use at most 64 MiB of HBM per device.

```python
import math
import jax
import jax.numpy as jnp
import numpy as np
from jax import lax

SLOTS = 128
STEPS = 2
ITERS = 4
NCX = 16
NCY = 32
NCZ = 8
BINS_Z = 16


def set_ends(values, own_key, least, high):
    index_at = [jax.random.randint(jax.random.fold_in(own_key, axis), (), 0, length) for axis, length in enumerate(values.shape)]
    main_axis = values.shape.index(max(values.shape))
    next_to = index_at[:main_axis] + [(index_at[main_axis] + 1) % values.shape[main_axis]] + index_at[main_axis + 1:]
    return values.at[tuple(index_at)].set(least).at[tuple(next_to)].set(high)


def block_levels(stream_key, dims, cuts, low, high):
    def one(dim, blocks):
        heights = jax.random.uniform(jax.random.fold_in(jax.random.fold_in(stream_key, 6), dim), (blocks,), jnp.float32, low / len(cuts), high / len(cuts))
        return jnp.repeat(jnp.exp(heights), dims[dim] // blocks).reshape((-1,) + (1,) * (len(dims) - dim - 1))

    gain = one(*cuts[0])
    for cut in cuts[1:]:
        gain = gain * one(*cut)
    return gain


def gaussian(key, shape, scale, bound, cuts=(), held_as=jnp.bfloat16):
    entries = jax.random.normal(key, shape, jnp.float32) * scale
    if len(cuts) > 0:
        entries = block_levels(key, shape, cuts, -0.22, 0.18) * entries
    return jnp.clip(entries, min=-bound, max=bound).astype(held_as)


def setup_inputs(seed: int = 0) -> dict:
    key_list = jax.random.split(jax.random.key(seed), 9)
    return {
        "bead_pos": jnp.clip(3.0 * jax.random.uniform(key_list[0], (3, NCX, NCY, NCZ, SLOTS), jnp.float32) ** block_levels(key_list[0], (3, NCX, NCY, NCZ, SLOTS), ((1, 8), (2, 8), (3, 4)), -0.2, 0.2), 0.0, 3.0),
        "bead_vel": gaussian(key_list[1], (3, NCX, NCY, NCZ, SLOTS), 1.0, 6.0, ((1, 8), (2, 8), (3, 4)), jnp.float32),
        "bead_force": gaussian(key_list[2], (3, NCX, NCY, NCZ, SLOTS), 10.0, 60.0, ((1, 8), (2, 8), (3, 4)), jnp.float32),
        "cell_count": set_ends(jax.random.randint(key_list[3], (NCX, NCY, NCZ), 0, SLOTS + 1), jax.random.fold_in(key_list[3], 1), 0, SLOTS).astype(jnp.int32),
        "pair_seed": set_ends(jax.random.randint(key_list[4], (NCX, NCY, NCZ, SLOTS), 0, 4096), jax.random.fold_in(key_list[4], 1), 0, 4095).astype(jnp.int32),
        "bead_half": set_ends(jax.random.randint(key_list[5], (NCX, NCY, NCZ, SLOTS), 0, 2), jax.random.fold_in(key_list[5], 1), 0, 1).astype(jnp.int32),
        "grid_vel": gaussian(key_list[6], (3, NCX, NCY, BINS_Z), 1.0, 6.0, ((1, 8), (2, 32)), jnp.float32),
        "correlation_map": set_ends((jax.random.randint(key_list[7], (NCX, NCY, BINS_Z), 0, 2) < 1).astype(jnp.int32), jax.random.fold_in(key_list[7], 1), 0, 1),
    }


cell_edge = 3.0
conserve = 25.0
friction = 4.5
noise_scale = 3.0 * math.sqrt(12.0) / math.sqrt(0.04)
time_step = 0.04
predict_weight = 0.65
couple_rate = 0.5
hash_prime = 4093

def pair_sum(center, padded, step_tag):
    extent_x, extent_y, extent_z = (center.shape[1], center.shape[2], center.shape[3])
    slot_count = center.shape[4]
    seed_own = center[6].astype(jnp.int32)[..., :, None]
    offsets_y = np.repeat(np.array([oy for oy in (-1, 0, 1) for oz in (-1, 0, 1)]), slot_count)
    offsets_z = np.repeat(np.array([oz for oy in (-1, 0, 1) for oz in (-1, 0, 1)]), slot_count)
    shift_y = jnp.asarray(offsets_y * cell_edge, dtype=jnp.float32)
    shift_z = jnp.asarray(offsets_z * cell_edge, dtype=jnp.float32)
    totals = [jnp.zeros(center.shape[1:], jnp.float32) for axis_k in range(3)]
    for offset_x in (-1, 0, 1):
        pieces = []
        for offset_y in (-1, 0, 1):
            for offset_z in (-1, 0, 1):
                pieces.append(padded[:, 1 + offset_x:1 + offset_x + extent_x, 1 + offset_y:1 + offset_y + extent_y, 1 + offset_z:1 + offset_z + extent_z, :])
        nearby = jnp.concatenate(pieces, axis=-1)
        shifts = (cell_edge * offset_x, shift_y, shift_z)
        deltas = [center[axis_k][..., :, None] - nearby[axis_k][..., None, :] - shifts[axis_k] for axis_k in range(3)]
        square = deltas[0] * deltas[0] + deltas[1] * deltas[1] + deltas[2] * deltas[2]
        weight = jnp.maximum(1.0 - square, 0.0) * nearby[7][..., None, :]
        closing = deltas[0] * (center[3][..., :, None] - nearby[3][..., None, :])
        closing = closing + deltas[1] * (center[4][..., :, None] - nearby[4][..., None, :])
        closing = closing + deltas[2] * (center[5][..., :, None] - nearby[5][..., None, :])
        seed_other = nearby[6].astype(jnp.int32)[..., None, :]
        hashed = jnp.remainder(seed_own * seed_other + (seed_own + seed_other) * step_tag, hash_prime)
        random_term = (hashed.astype(jnp.float32) / hash_prime - 0.5) * noise_scale
        strength = weight * (conserve + random_term) - friction * weight * weight * closing
        for axis_k in range(3):
            totals[axis_k] = totals[axis_k] + lax.optimization_barrier(jnp.sum(strength * deltas[axis_k], axis=-1))
    return jnp.stack(totals) * center[7]

def pad_domain(field):
    wrapped = jnp.pad(field, [(0, 0), (1, 1)] + [(0, 0)] * (field.ndim - 2), mode='wrap')
    return jnp.pad(wrapped, [(0, 0), (0, 0), (1, 1), (1, 1)] + [(0, 0)] * (field.ndim - 4))

def all_forces(stacked, step_tag):
    padded = pad_domain(stacked)

    def plane(index):
        block_rows = lax.dynamic_slice_in_dim(padded, index, 3, 1)
        return pair_sum(block_rows[:, 1:2, 1:-1, 1:-1], block_rows, step_tag)[:, 0]
    planes = lax.map(plane, jnp.arange(NCX, dtype=jnp.int32))
    return jnp.moveaxis(planes, 0, 1)

def bin_sums(velocity, occupied, bead_half):
    pieces = []
    for side_index in (0, 1):
        select = occupied * (bead_half == side_index).astype(jnp.float32)
        moments = lax.optimization_barrier(jnp.sum(velocity * select[None], axis=-1))
        counted = lax.optimization_barrier(jnp.sum(select, axis=-1))
        pieces.append(jnp.concatenate([moments, counted[None]], axis=0))
    joined = jnp.stack(pieces, axis=-1)
    extent = joined.shape
    return joined.reshape(extent[0], extent[1], extent[2], extent[3] * 2)

def couple(bin_totals, grid_field, coupled_flag):
    bin_mean = bin_totals[:3] / jnp.maximum(bin_totals[3], 1.0)
    return grid_field + couple_rate * coupled_flag * (bin_mean - grid_field)

def project(coupled_vel, pad, reduce_all):
    padded = pad(coupled_vel)
    divergence = padded[0, 2:, 1:-1, 1:-1] - padded[0, :-2, 1:-1, 1:-1]
    divergence = divergence + padded[1, 1:-1, 2:, 1:-1] - padded[1, 1:-1, :-2, 1:-1]
    divergence = 0.5 * (divergence + padded[2, 1:-1, 1:-1, 2:] - padded[2, 1:-1, 1:-1, :-2])

    def operate(field):
        beside_all = pad(field[None])[0]
        beside = beside_all[2:, 1:-1, 1:-1] + beside_all[:-2, 1:-1, 1:-1]
        beside = beside + beside_all[1:-1, 2:, 1:-1] + beside_all[1:-1, :-2, 1:-1]
        beside = beside + beside_all[1:-1, 1:-1, 2:] + beside_all[1:-1, 1:-1, :-2]
        return 6.0 * field - beside
    residual = -divergence
    direction = residual
    pressure = jnp.zeros_like(residual)
    norm_now = reduce_all(residual * residual)
    for repeat in range(ITERS):
        applied = operate(direction)
        step_length = norm_now / reduce_all(direction * applied)
        pressure = pressure + step_length * direction
        residual = residual - step_length * applied
        norm_next = reduce_all(residual * residual)
        direction = residual + norm_next / norm_now * direction
        norm_now = norm_next
    beside_all = pad(pressure[None])[0]
    gradient = jnp.stack([beside_all[2:, 1:-1, 1:-1] - beside_all[:-2, 1:-1, 1:-1], beside_all[1:-1, 2:, 1:-1] - beside_all[1:-1, :-2, 1:-1], beside_all[1:-1, 1:-1, 2:] - beside_all[1:-1, 1:-1, :-2]])
    return (coupled_vel - 0.5 * gradient, pressure)

def reference(bead_pos, bead_vel, bead_force, cell_count, pair_seed, bead_half, grid_vel, correlation_map):
    occupied = (lax.broadcasted_iota(jnp.int32, pair_seed.shape, 3) < cell_count[..., None]).astype(jnp.float32)
    static = jnp.stack([pair_seed.astype(jnp.float32), occupied])
    position, velocity, current = (bead_pos, bead_vel, bead_force)
    for step_number in range(STEPS):
        step_tag = step_number + 3
        position = position + time_step * velocity + 0.5 * time_step * time_step * current
        guessed = velocity + predict_weight * time_step * current
        predicted = all_forces(jnp.concatenate([position, guessed, static]), step_tag)
        corrected = velocity + 0.5 * time_step * (current + predicted)
        iterated = all_forces(jnp.concatenate([position, corrected, static]), step_tag)
        velocity = velocity + 0.5 * time_step * (current + iterated)
        current = iterated
    bin_totals = bin_sums(velocity, occupied, bead_half)
    coupled_vel = couple(bin_totals, grid_vel, correlation_map.astype(jnp.float32))
    grid_velocity, pressure = project(coupled_vel, pad_domain, jnp.sum)
    return (position, velocity, grid_velocity, pressure, grid_velocity)
```

```python
import math

import jax
import jax.numpy as jnp
from jax import lax
from jax.experimental import pallas as pl
from jax.experimental.pallas import tpu as pltpu
from jax.sharding import PartitionSpec as P

STEPS = 2
ITERS = 4

cell_edge = 3.0
conserve = 25.0
friction = 4.5
noise_scale = 3.0 * math.sqrt(12.0) / math.sqrt(0.04)
time_step = 0.04
predict_weight = 0.65
couple_rate = 0.5
hash_prime = 4093.0

ROUND = 12582912.0
SLOTS = 128
IB = 32
NFEAT = 64
HX, HY, HZ = 4, 6, 4
FAR = 1.0e5
damp = -friction / noise_scale
lift = conserve / noise_scale - 0.5 / hash_prime


def rint(value):
    return (value + ROUND) - ROUND


def split3(value):
    hi = value.astype(jnp.bfloat16).astype(jnp.float32)
    rest = value - hi
    mid = rest.astype(jnp.bfloat16).astype(jnp.float32)
    low = (rest - mid).astype(jnp.bfloat16).astype(jnp.float32)
    return hi, mid, low


def rows_of(row, values, default):
    out = default
    for index, value in values:
        out = jnp.where(row == index, value, out)
    return out


def bead_tile(raw, off, row):
    x = raw[0:1] + off[0]
    y = raw[1:2] + off[1]
    z = raw[2:3] + off[2]
    vx = raw[3:4] * damp
    vy = raw[4:5] * damp
    vz = raw[5:6] * damp
    q = x * x + y * y + z * z
    p = x * vx + y * vy + z * vz
    q = jnp.where(raw[7:8] > 0.5, q, FAR)
    return x, y, z, vx, vy, vz, q, p


def centred(seed, tag):
    a = seed + tag
    return jnp.where(a > 2046.0, a - hash_prime, a)


def force_kernel(tag, mode, count_ref, own, zlo, zhi, ylo, yhi, xlo, xhi, *rest):
    if mode == "predict":
        vf, out, feat, posb, left, acc = rest
    elif mode == "step":
        vf, out, vf_out, feat, posb, left, acc = rest
    else:
        vf, half, pos_out, vel_out, bins_out, feat, posb, left, acc = rest
    row8 = lax.broadcasted_iota(jnp.int32, (8, SLOTS), 0)
    row16 = lax.broadcasted_iota(jnp.int32, (16, SLOTS), 0)

    def features(raw, hx, hy, hz):
        off = (
            (hx * 3 - 6).astype(jnp.float32),
            (hy * 3 - 9).astype(jnp.float32),
            (hz * 3 - 6).astype(jnp.float32),
        )
        x, y, z, vx, vy, vz, q, p = bead_tile(raw, off, row8)
        tile = jnp.concatenate([x, y, z, vx, vy, vz, q, p], axis=0)
        hi, mid, low = split3(tile)
        a = centred(raw[6:7], tag)
        c = rint(a * (1.0 / 64.0))
        d = a - 64.0 * c
        fixed = jnp.where(
            row16 < 3, c, jnp.where(row16 < 6, d, jnp.where(row16 < 9, 1.0, 0.0))
        )
        both = jnp.concatenate([hi, mid, hi, low, hi, mid, fixed], axis=0)
        column = pl.multiple_of(((hx * HY + hy) * HZ + hz) * SLOTS, SLOTS)
        feat[:, pl.ds(column, SLOTS)] = both.astype(jnp.bfloat16)
        posb[:, pl.ds(column, SLOTS)] = jnp.concatenate(
            [
                jnp.broadcast_to(x, (8, SLOTS)),
                jnp.broadcast_to(y, (8, SLOTS)),
                jnp.broadcast_to(z, (8, SLOTS)),
            ],
            axis=0,
        )
        return hi, mid, low, tile, a

    def of_own(index, carry):
        hx, hy, hz = index // 8, (index // 2) % 4, index % 2
        raw = own[index]
        hi, mid, low, tile, a = features(raw, hx + 1, hy + 1, hz + 1)
        zero = jnp.zeros((1, SLOTS), jnp.float32)
        one = jnp.ones((1, SLOTS), jnp.float32)

        def s_group(part, last):
            return jnp.concatenate([2.0 * part[0:3], zero, zero, zero, last, zero], axis=0)

        def c_group(part, last):
            return jnp.concatenate([-part[3:6], -part[0:3], zero, last], axis=0)

        x, y, z = tile[0:1], tile[1:2], tile[2:3]
        g3 = split3(1.0 - (x * x + y * y + z * z))
        e3 = split3(tile[7:8])
        a64 = 64.0 * a
        a64 = a64 - hash_prime * rint(a64 * (1.0 / hash_prime))
        b64 = split3(a64 / hash_prime)
        b1 = split3(a / hash_prime)
        shift = split3(jnp.full((1, SLOTS), (0.5 - tag * tag) / hash_prime - 0.5, jnp.float32))
        pad7 = jnp.zeros((7, SLOTS), jnp.float32)
        pad6 = jnp.zeros((6, SLOTS), jnp.float32)
        left_s = jnp.concatenate(
            [
                s_group(hi, -one),
                s_group(hi, -one),
                s_group(mid, zero),
                s_group(hi, -one),
                s_group(low, zero),
                s_group(mid, zero),
                pad6,
                g3[0],
                g3[1],
                g3[2],
                pad7,
            ],
            axis=0,
        )
        left_c = jnp.concatenate(
            [
                c_group(hi, one),
                c_group(hi, one),
                c_group(mid, zero),
                c_group(hi, one),
                c_group(low, zero),
                c_group(mid, zero),
                pad6,
                e3[0],
                e3[1],
                e3[2],
                pad7,
            ],
            axis=0,
        )
        left_u = jnp.concatenate(
            [
                jnp.zeros((48, SLOTS), jnp.float32),
                b64[0],
                b64[1],
                b64[2],
                b1[0],
                b1[1],
                b1[2],
                shift[0],
                shift[1],
                shift[2],
                pad7,
            ],
            axis=0,
        )
        for which, rows in enumerate((left_s, left_c, left_u)):
            turned = rows.T.astype(jnp.bfloat16)
            for block in range(SLOTS // IB):
                start = pl.multiple_of(index * (3 * SLOTS) + (block * 3 + which) * IB, IB)
                left[pl.ds(start, IB), :] = turned[block * IB : (block + 1) * IB]
        return carry

    lax.fori_loop(0, 16, of_own, 0)

    def of_face(ref, count, place):
        def body(index, carry):
            features(ref[index], *place(index))
            return carry

        lax.fori_loop(0, count, body, 0, unroll=2)

    def fixed(value, like):
        return like * 0 + value

    of_face(zlo, 8, lambda i: (i // 4 + 1, i % 4 + 1, fixed(0, i)))
    of_face(zhi, 8, lambda i: (i // 4 + 1, i % 4 + 1, fixed(3, i)))
    of_face(ylo, 8, lambda i: (i // 4 + 1, fixed(0, i), i % 4))
    of_face(yhi, 8, lambda i: (i // 4 + 1, fixed(5, i), i % 4))
    of_face(xlo, 24, lambda i: (fixed(0, i), i // 4, i % 4))
    of_face(xhi, 24, lambda i: (fixed(3, i), i // 4, i % 4))

    def of_cell(index, carry):
        cx, cy, cz = index // 8, (index // 2) % 4, index % 2
        n_own = count_ref[index]
        acc[...] = jnp.zeros_like(acc)

        def of_block(block, inner):
            start = pl.multiple_of(index * (3 * SLOTS) + block * (3 * IB), 3 * IB)
            lhs = left[pl.ds(start, 3 * IB), :]
            sums = [jnp.zeros((IB, SLOTS), jnp.float32) for _ in range(4)]
            columns = [
                pl.multiple_of(
                    (((cx + ox) * HY + (cy + oy)) * HZ + cz) * SLOTS, SLOTS
                )
                for ox in range(3)
                for oy in range(3)
            ]
            groups = [columns[0:2], columns[2:4], columns[4:6], columns[6:8], columns[8:9]]
            for group in groups:
                rhs = jnp.concatenate([feat[:, pl.ds(c, 3 * SLOTS)] for c in group], axis=1)
                forms = jnp.dot(lhs, rhs, preferred_element_type=jnp.float32)
                for piece in range(len(group) * 3):
                    lanes = slice(piece * SLOTS, (piece + 1) * SLOTS)
                    s = forms[0:IB, lanes]
                    damped = forms[IB : 2 * IB, lanes]
                    u = forms[2 * IB : 3 * IB, lanes]
                    weight = jnp.maximum(s, 0.0)
                    strength = weight * ((u - rint(u)) + lift + weight * damped)
                    where = group[piece // 3] + (piece % 3) * SLOTS
                    here = posb[:, pl.ds(pl.multiple_of(where, SLOTS), SLOTS)]
                    for k in range(3):
                        wide = jnp.concatenate([here[8 * k : 8 * k + 8]] * (IB // 8), axis=0)
                        sums[k] = sums[k] + strength * wide
                    sums[3] = sums[3] + strength
            for k in range(4):
                acc[k, pl.ds(pl.multiple_of(block * IB, IB), IB), :] = sums[k]
            return inner

        lax.fori_loop(0, (n_own + (IB - 1)) // IB, of_block, 0)
        moments = [jnp.sum(acc[k].T, axis=0, keepdims=True) for k in range(4)]
        raw = own[index]
        occupied = raw[7:8]
        off = (
            (cx * 3 - 3).astype(jnp.float32),
            (cy * 3 - 6).astype(jnp.float32),
            (cz * 3 - 3).astype(jnp.float32),
        )
        total = [
            noise_scale * occupied * ((raw[k : k + 1] + off[k]) * moments[3] - moments[k])
            for k in range(3)
        ]
        state = vf[index]
        v = [state[k : k + 1] for k in range(3)]
        f = [state[k + 3 : k + 4] for k in range(3)]
        new_v = [v[k] + 0.5 * time_step * (f[k] + total[k]) for k in range(3)]
        if mode == "predict":
            out[index] = jnp.concatenate([raw[0:3], *new_v, raw[6:8]], axis=0)
        elif mode == "step":
            moved = [
                raw[k : k + 1] + time_step * new_v[k] + 0.5 * time_step * time_step * total[k]
                for k in range(3)
            ]
            guess = [new_v[k] + predict_weight * time_step * total[k] for k in range(3)]
            out[index] = jnp.concatenate([*moved, *guess, raw[6:8]], axis=0)
            vf_out[index] = jnp.concatenate([*new_v, *total, raw[6:8]], axis=0)
        else:
            for k in range(3):
                pos_out[k, cx, cy, pl.ds(cz, 1), :] = raw[k : k + 1]
                vel_out[k, cx, cy, pl.ds(cz, 1), :] = new_v[k]
            side = half[cx, cy, pl.ds(cz, 1), :]
            rows = []
            for h in (0, 1):
                select = jnp.where(side == h, occupied, 0.0)
                rows += [new_v[0] * select, new_v[1] * select, new_v[2] * select, select]
            summed = jnp.sum(jnp.concatenate(rows, axis=0), axis=1, keepdims=True)
            lane = lax.broadcasted_iota(jnp.int32, (8, SLOTS), 1)
            bins_out[...] = jnp.where(lane == index, summed, bins_out[...])
        return carry

    if mode == "last":
        bins_out[...] = jnp.zeros_like(bins_out)
    lax.fori_loop(0, 16, of_cell, 0)


def force_call(tag, mode, counts, own, faces, *extra):
    tile = jax.ShapeDtypeStruct((16, 8, SLOTS), jnp.float32)
    bead = jax.ShapeDtypeStruct((3, 2, 4, 2, SLOTS), jnp.float32)
    shapes = {
        "predict": tile,
        "step": (tile, tile),
        "last": (bead, bead, jax.ShapeDtypeStruct((8, SLOTS), jnp.float32)),
    }[mode]
    vmem = pl.BlockSpec(memory_space=pltpu.VMEM)
    n_out = 1 if mode == "predict" else len(shapes)

    def body(*refs):
        force_kernel(float(tag), mode, *refs)

    return pl.pallas_call(
        body,
        out_shape=shapes,
        in_specs=[pl.BlockSpec(memory_space=pltpu.SMEM)] + [vmem] * (7 + len(extra)),
        out_specs=vmem if n_out == 1 else tuple([vmem] * n_out),
        scratch_shapes=[
            pltpu.VMEM((NFEAT, HX * HY * HZ * SLOTS), jnp.bfloat16),
            pltpu.VMEM((24, HX * HY * HZ * SLOTS), jnp.float32),
            pltpu.VMEM((16 * 3 * SLOTS, NFEAT), jnp.bfloat16),
            pltpu.VMEM((4, SLOTS, SLOTS), jnp.float32),
        ],
        cost_estimate=pl.CostEstimate(
            flops=10_000_000, bytes_accessed=1_000_000, transcendentals=0
        ),
        name="pair_" + mode,
    )(counts, own, *faces, *extra)


def shifted(block, axis, periodic, up):
    count = lax.axis_size(axis)
    pairs = [(i, i + 1) for i in range(count - 1)]
    if periodic:
        pairs.append((count - 1, 0))
    if not up:
        pairs = [(b, a) for a, b in pairs]
    return lax.ppermute(block, axis, pairs)


def gather_faces(own):
    zlo = shifted(own[:, :, 1:2], "gz", False, True)
    zhi = shifted(own[:, :, 0:1], "gz", False, False)
    wide_z = jnp.concatenate([zlo, own, zhi], axis=2)
    ylo = shifted(wide_z[:, 3:4], "gy", False, True)
    yhi = shifted(wide_z[:, 0:1], "gy", False, False)
    wide_y = jnp.concatenate([ylo, wide_z, yhi], axis=1)
    xlo = shifted(wide_y[1:2], "gx", True, True)
    xhi = shifted(wide_y[0:1], "gx", True, False)
    return tuple(face.reshape(-1, 8, SLOTS) for face in (zlo, zhi, ylo, yhi, xlo, xhi))


def neighbours(field):
    nx = jnp.roll(field, -1, axis=-3)
    px = jnp.roll(field, 1, axis=-3)
    wide = jnp.pad(field, [(0, 0)] * (field.ndim - 2) + [(1, 1), (1, 1)])
    ny = wide[..., 2:, 1:-1]
    py = wide[..., :-2, 1:-1]
    nz = wide[..., 1:-1, 2:]
    pz = wide[..., 1:-1, :-2]
    return nx, px, ny, py, nz, pz


def project(coupled):
    near = [neighbours(coupled[k]) for k in range(3)]
    residual = -0.5 * (
        near[0][0] - near[0][1] + near[1][2] - near[1][3] + near[2][4] - near[2][5]
    )
    direction = residual
    pressure = jnp.zeros_like(residual)
    norm_now = jnp.sum(residual * residual)
    for repeat in range(ITERS):
        around = neighbours(direction)
        applied = 6.0 * direction - sum(around[1:], around[0])
        step_length = norm_now / jnp.sum(direction * applied)
        pressure = pressure + step_length * direction
        residual = residual - step_length * applied
        norm_next = jnp.sum(residual * residual)
        direction = residual + norm_next / norm_now * direction
        norm_now = norm_next
    nx, px, ny, py, nz, pz = neighbours(pressure)
    gradient = jnp.stack([nx - px, ny - py, nz - pz])
    return coupled - 0.5 * gradient, pressure


def per_device(
    bead_pos, bead_vel, bead_force, cell_count, pair_seed, bead_half, grid_vel, correlation_map
):
    occupied = (lax.broadcasted_iota(jnp.int32, pair_seed.shape, 3) < cell_count[..., None]).astype(
        jnp.float32
    )
    seed = pair_seed.astype(jnp.float32)
    position = bead_pos + time_step * bead_vel + 0.5 * time_step * time_step * bead_force
    guessed = bead_vel + predict_weight * time_step * bead_force
    static = jnp.stack([seed, occupied])
    tiles = jnp.moveaxis(jnp.concatenate([position, guessed, static]), 0, -2)
    state = jnp.moveaxis(jnp.concatenate([bead_vel, bead_force, static]), 0, -2)
    state = state.reshape(16, 8, SLOTS)
    counts = cell_count.reshape(16)
    shape = (2, 4, 2, 8, SLOTS)

    for step in range(STEPS):
        tag = step + 3
        tiles = force_call(
            tag, "predict", counts, tiles.reshape(16, 8, SLOTS), gather_faces(tiles), state
        ).reshape(shape)
        if step < STEPS - 1:
            tiles, state = force_call(
                tag, "step", counts, tiles.reshape(16, 8, SLOTS), gather_faces(tiles), state
            )
            tiles = tiles.reshape(shape)
        else:
            position, velocity, bins = force_call(
                tag,
                "last",
                counts,
                tiles.reshape(16, 8, SLOTS),
                gather_faces(tiles),
                state,
                bead_half,
            )
    sent = jnp.concatenate(
        [
            bins[:, :16].reshape(-1),
            grid_vel.reshape(-1),
            correlation_map.astype(jnp.float32).reshape(-1),
        ]
    )
    nx, ny, nz = (lax.axis_size(a) for a in ("gx", "gy", "gz"))
    world = nx * ny * nz
    got = lax.all_to_all(
        jnp.broadcast_to(sent[None], (world, 256)), ("gx", "gy", "gz"), 0, 0, tiled=True
    )
    bin_all = got[:, :128].reshape(nx, ny, nz, 2, 4, 2, 4, 2)
    bin_all = bin_all.transpose(4, 0, 5, 1, 6, 2, 7, 3).reshape(4, 16, 32, 16)
    grid_all = got[:, 128:224].reshape(nx, ny * nz, 3, 2, 16).transpose(2, 0, 3, 1, 4)
    grid_all = grid_all.reshape(3, 16, 32, 16)
    flag_all = got[:, 224:].reshape(nx, ny * nz, 2, 16).transpose(0, 2, 1, 3).reshape(16, 32, 16)
    mean = bin_all[:3] / jnp.maximum(bin_all[3], 1.0)
    coupled = grid_all + couple_rate * flag_all * (mean - grid_all)
    velocity_all, pressure_all = project(coupled)
    ix, iy, iz = (lax.axis_index(a) for a in ("gx", "gy", "gz"))
    grid_velocity = lax.dynamic_slice(
        velocity_all, (0, 2 * ix, iy * nz + iz, 0), (3, 2, 1, 16)
    )
    pressure = lax.dynamic_slice(pressure_all, (2 * ix, iy * nz + iz, 0), (2, 1, 16))
    brick = lax.dynamic_slice(velocity_all, (0, 2 * ix, 4 * iy, 4 * iz), (3, 2, 4, 4))
    return (position, velocity, grid_velocity, pressure, brick)


def solution(mesh):
    placed = (
        P(None, "gx", "gy", "gz", None),
        P(None, "gx", "gy", "gz", None),
        P(None, "gx", "gy", "gz", None),
        P("gx", "gy", "gz"),
        P("gx", "gy", "gz", None),
        P("gx", "gy", "gz", None),
        P(None, "gx", ("gy", "gz"), None),
        P("gx", ("gy", "gz"), None),
    )
    return jax.shard_map(
        per_device,
        mesh=mesh,
        in_specs=placed,
        out_specs=(
            P(None, "gx", "gy", "gz", None),
            P(None, "gx", "gy", "gz", None),
            P(None, "gx", ("gy", "gz"), None),
            P("gx", ("gy", "gz"), None),
            P(None, "gx", "gy", "gz"),
        ),
        check_vma=False,
    )
```

```python
import math

import jax
import jax.numpy as jnp
from jax import lax
from jax.experimental import pallas as pl
from jax.experimental.pallas import tpu as pltpu
from jax.sharding import PartitionSpec as P

STEPS = 2
ITERS = 4

cell_edge = 3.0
conserve = 25.0
friction = 4.5
noise_scale = 3.0 * math.sqrt(12.0) / math.sqrt(0.04)
time_step = 0.04
predict_weight = 0.65
couple_rate = 0.5
hash_prime = 4093.0

ROUND = 12582912.0
SLOTS = 128
IB = 16
ROWS = 192
NFEAT = 64
HX, HY, HZ = 4, 3, 10
CELLS = HX * HY * HZ
ITEMS = 16 * (ROWS // IB) + 8
RUN = 4
FAR = 1.0e5
damp = -friction / noise_scale
lift = conserve / noise_scale - 0.5 / hash_prime


def rint(value):
    return (value + ROUND) - ROUND


def split3(value):
    hi = value.astype(jnp.bfloat16).astype(jnp.float32)
    rest = value - hi
    mid = rest.astype(jnp.bfloat16).astype(jnp.float32)
    low = (rest - mid).astype(jnp.bfloat16).astype(jnp.float32)
    return hi, mid, low


def rows_of(row, values, default):
    out = default
    for index, value in values:
        out = jnp.where(row == index, value, out)
    return out


def bead_tile(raw, off, row):
    x = raw[0:1] + off[0]
    y = raw[1:2] + off[1]
    z = raw[2:3] + off[2]
    vx = raw[3:4] * damp
    vy = raw[4:5] * damp
    vz = raw[5:6] * damp
    q = x * x + y * y + z * z
    p = x * vx + y * vy + z * vz
    q = jnp.where(raw[7:8] > 0.5, q, FAR)
    return x, y, z, vx, vy, vz, q, p


def centred(seed, tag):
    a = seed + tag
    return jnp.where(a > 2046.0, a - hash_prime, a)


def force_kernel(tag, mode, own, ylo, yhi, xlo, xhi, *rest):
    if mode == "predict":
        vf, out, *scratch = rest
    elif mode == "step":
        vf, out, vf_out, *scratch = rest
    else:
        vf, out, bins_out, *scratch = rest
    feat, posb, left, perm, acc, form_a, items, held_at = scratch
    row8 = lax.broadcasted_iota(jnp.int32, (8, SLOTS), 0)
    row16 = lax.broadcasted_iota(jnp.int32, (16, SLOTS), 0)

    def brick_offset(hx, hy, hz):
        return (
            (hx * 3 - 6).astype(jnp.float32),
            (hy * 3).astype(jnp.float32) - 4.5,
            (hz * 3 - 15).astype(jnp.float32),
        )

    def features(raw, place, bounds):
        hx, hy, hz = place
        tile = jnp.concatenate(bead_tile(raw, brick_offset(hx, hy, hz), row8), axis=0)
        hi, mid, low = split3(tile)
        a = centred(raw[6:7], tag)
        c = rint(a * (1.0 / 64.0))
        d = a - 64.0 * c
        fixed = jnp.where(
            row16 < 3, c, jnp.where(row16 < 6, d, jnp.where(row16 < 9, 1.0, 0.0))
        )
        both = jnp.concatenate([hi, mid, hi, low, hi, mid, fixed], axis=0)
        column = pl.multiple_of(((hx * HY + hy) * HZ + hz) * SLOTS, SLOTS)
        feat[:, pl.ds(column, SLOTS)] = both.astype(jnp.bfloat16)
        posb[:, pl.ds(column, SLOTS)] = jnp.concatenate(
            [jnp.broadcast_to(tile[k : k + 1], (8, SLOTS)) for k in range(3)], axis=0
        )
        there = jnp.where(raw[7:8] > 0.5, raw, 0.5 * cell_edge)
        return (jnp.minimum(bounds[0], there), jnp.maximum(bounds[1], there))

    def of_face(ref, count, place, bounds):
        def body(index, carry):
            return features(ref[index], place(index), carry)

        return lax.fori_loop(0, count, body, bounds, unroll=4)

    def fixed_at(value, like):
        return like * 0 + value

    middle = jnp.full((8, SLOTS), 0.5 * cell_edge, jnp.float32)
    bounds = (middle, middle)
    bounds = of_face(own, 16, lambda i: (i // 8 + 1, fixed_at(1, i), i % 8 + 1), bounds)
    bounds = of_face(ylo, 16, lambda i: (i // 8 + 1, fixed_at(0, i), i % 8 + 1), bounds)
    bounds = of_face(yhi, 16, lambda i: (i // 8 + 1, fixed_at(2, i), i % 8 + 1), bounds)
    bounds = of_face(xlo, 24, lambda i: (fixed_at(0, i), i // 8, i % 8 + 1), bounds)
    bounds = of_face(xhi, 24, lambda i: (fixed_at(3, i), i // 8, i % 8 + 1), bounds)
    nothing = jnp.where(lax.broadcasted_iota(jnp.int32, (NFEAT, SLOTS), 0) == 6, FAR, 0.0)
    nothing = nothing.astype(jnp.bfloat16)
    for column in range(HX * HY):
        for end in (0, HZ - 1):
            at = (column * HZ + end) * SLOTS
            feat[:, at : at + SLOTS] = nothing
            posb[:, at : at + SLOTS] = jnp.zeros((24, SLOTS), jnp.float32)
    least = jnp.min(bounds[0], axis=1, keepdims=True)
    most = jnp.max(bounds[1], axis=1, keepdims=True)
    cut = 0.5 * (least + most)
    span = jnp.maximum(most[0:1] - least[0:1], most[1:2] - least[1:2])
    apart = jnp.where(span < 3.99, 1.0, 0.0)

    before = jnp.where(
        lax.broadcasted_iota(jnp.int32, (SLOTS, SLOTS), 0)
        < lax.broadcasted_iota(jnp.int32, (SLOTS, SLOTS), 1),
        1.0,
        0.0,
    ).astype(jnp.bfloat16)
    place_row = lax.broadcasted_iota(jnp.int32, (ROWS, SLOTS), 0).astype(jnp.float32)

    lane1 = lax.broadcasted_iota(jnp.int32, (1, SLOTS), 1)

    def of_own(index, codes):
        raw = own[index]
        off = brick_offset(index // 8 + 1, index * 0 + 1, index % 8 + 1)
        tile = jnp.concatenate(bead_tile(raw, off, row8), axis=0)
        hi, mid, low = split3(tile)
        a = centred(raw[6:7], tag)
        zero = jnp.zeros((1, SLOTS), jnp.float32)
        one = jnp.ones((1, SLOTS), jnp.float32)

        def s_group(part, last):
            return jnp.concatenate([2.0 * part[0:3], zero, zero, zero, last, zero], axis=0)

        def c_group(part, last):
            return jnp.concatenate([-part[3:6], -part[0:3], zero, last], axis=0)

        x, y, z = tile[0:1], tile[1:2], tile[2:3]
        g3 = split3(1.0 - (x * x + y * y + z * z))
        e3 = split3(tile[7:8])
        a64 = 64.0 * a
        a64 = a64 - hash_prime * rint(a64 * (1.0 / hash_prime))
        b64 = split3(a64 * (1.0 / hash_prime))
        b1 = split3(a * (1.0 / hash_prime))
        shift = split3(jnp.full((1, SLOTS), (0.5 - tag * tag) / hash_prime - 0.5, jnp.float32))
        pad7 = jnp.zeros((7, SLOTS), jnp.float32)
        pad6 = jnp.zeros((6, SLOTS), jnp.float32)
        left_s = jnp.concatenate(
            [
                s_group(hi, -one),
                s_group(hi, -one),
                s_group(mid, zero),
                s_group(hi, -one),
                s_group(low, zero),
                s_group(mid, zero),
                pad6,
                *g3,
                pad7,
            ],
            axis=0,
        )
        left_c = jnp.concatenate(
            [
                c_group(hi, one),
                c_group(hi, one),
                c_group(mid, zero),
                c_group(hi, one),
                c_group(low, zero),
                c_group(mid, zero),
                pad6,
                *e3,
                pad7,
            ],
            axis=0,
        )
        left_u = jnp.concatenate(
            [jnp.zeros((48, SLOTS), jnp.float32), *b64, *b1, *shift, pad7], axis=0
        )
        occupied = jnp.where(raw[7:8] > 0.5, 1.0, 0.0)
        side_x = jnp.where(raw[0:1] > cut[0:1], apart, 0.0)
        side_y = jnp.where(raw[1:2] > cut[1:2], apart, 0.0)
        quarter = 2.0 * side_x + side_y
        masks = jnp.concatenate(
            [jnp.where(quarter == float(g), occupied, 0.0) for g in range(4)]
            + [jnp.zeros((4, SLOTS), jnp.float32)],
            axis=0,
        )
        rank = jnp.dot(masks.astype(jnp.bfloat16), before, preferred_element_type=jnp.float32)
        held = jnp.sum(masks, axis=1, keepdims=True)
        blocks = jnp.floor((held + (IB - 1.0)) * (1.0 / IB))
        first = [jnp.zeros((1, 1), jnp.float32)]
        for g in range(3):
            first.append(first[-1] + blocks[g : g + 1])
        slot = jnp.full((1, SLOTS), -1.0, jnp.float32)
        for g in range(4):
            here = float(IB) * first[g] + rank[g : g + 1]
            slot = jnp.where(masks[g : g + 1] > 0.5, here, slot)
        chosen = jnp.where(place_row == slot, 1.0, 0.0).astype(jnp.bfloat16)
        perm[index] = chosen
        for which, rows in enumerate((left_s, left_c, left_u)):
            turned = rows.T.astype(jnp.bfloat16)
            ordered = jnp.dot(chosen, turned, preferred_element_type=jnp.float32)
            ordered = ordered.astype(jnp.bfloat16)
            for block in range(ROWS // IB):
                start = pl.multiple_of(index * (3 * ROWS) + (block * 3 + which) * IB, IB)
                left[pl.ds(start, IB), :] = ordered[block * IB : (block + 1) * IB]
        code = blocks[0:1] + 16.0 * blocks[1:2] + 256.0 * blocks[2:3] + 4096.0 * blocks[3:4]
        return jnp.where(lane1 == index, code, codes)

    codes = lax.fori_loop(0, 16, of_own, jnp.zeros((1, SLOTS), jnp.float32), unroll=4)
    codes = jnp.where(lane1 == 16, apart, codes).astype(jnp.int32)
    for k in range(17):
        held_at[k] = codes[0, k]

    def list_cell(index, n_items):
        code = held_at[index]
        corner = (index // 8) * (HY * HZ) + index % 8
        row = index * (ROWS // IB) * SLOTS
        for g in range(4):
            first = row + corner + (g // 2) * (HY * HZ) + (g % 2) * HZ

            def put(b, at, first=first):
                items[at] = first + b * SLOTS
                return at + 1

            here = (code >> (4 * g)) & 15
            n_items = lax.fori_loop(0, here, put, n_items)
            row = row + here * SLOTS
        return n_items

    n_items = lax.fori_loop(0, 16, list_cell, jnp.int32(0))
    for extra in range(5):
        items[n_items + extra] = 16 * (ROWS // IB) * SLOTS

    acc[...] = jnp.zeros_like(acc)
    lane16 = lax.broadcasted_iota(jnp.int32, (IB, SLOTS), 1)

    def span_of(item):
        block, cell = item // SLOTS, item % SLOTS
        columns = [cell, cell + HZ, cell + HY * HZ, cell + (HY + 1) * HZ]
        return block, [pl.multiple_of(c * SLOTS, SLOTS) for c in columns]

    wide3 = 3 * SLOTS

    def multiply(block, columns, form, k):
        row = pl.multiple_of(block * (3 * IB), 3 * IB)
        rhs = [feat[:, pl.ds(c, wide3)] for c in columns]
        rhs = rhs[0] if len(rhs) == 1 else jnp.concatenate(rhs, axis=1)
        form[:, k * wide3 : k * wide3 + rhs.shape[1]] = jnp.dot(
            left[pl.ds(row, 3 * IB), :], rhs, preferred_element_type=jnp.float32
        )

    def combine(column, form, k, sums):
        sums = list(sums)
        for piece in range(3):
            lanes = slice((3 * k + piece) * SLOTS, (3 * k + piece + 1) * SLOTS)
            weight = jnp.maximum(form[0:IB, lanes], 0.0)
            u = form[2 * IB : 3 * IB, lanes]
            strength = weight * ((u - rint(u)) + lift + weight * form[IB : 2 * IB, lanes])
            here = posb[:, pl.ds(pl.multiple_of(column + piece * SLOTS, SLOTS), SLOTS)]
            for d in range(3):
                wide = jnp.concatenate([here[8 * d : 8 * d + 8]] * (IB // 8), axis=0)
                sums[d] = sums[d] + strength * wide
            sums[3] = sums[3] + strength
        return sums

    def finish(block, sums):
        gathered = jnp.zeros((IB, SLOTS), jnp.float32)
        for d in range(4):
            whole = jnp.sum(sums[d], axis=1, keepdims=True)
            gathered = jnp.where(lane16 == d, whole, gathered)
        row = pl.multiple_of(block * IB, IB)
        acc[pl.ds(row, IB), :] = acc[pl.ds(row, IB), :] + gathered

    @pl.when(held_at[16] == 1)
    def _():
        block, columns = span_of(items[0])
        for k in (0, 2):
            multiply(block, columns[k : k + 2], form_a, k)

        def of_run(index, carry):
            spans = [span_of(items[RUN * index + k]) for k in range(RUN + 1)]
            for turn in range(RUN):
                block, columns = spans[turn]
                later_block, later_columns = spans[turn + 1]
                sums = [jnp.zeros((IB, SLOTS), jnp.float32) for _ in range(4)]
                for k in (0, 2):
                    sums = combine(columns[k], form_a, k, sums)
                    sums = combine(columns[k + 1], form_a, k + 1, sums)
                    multiply(later_block, later_columns[k : k + 2], form_a, k)
                finish(block, sums)
            return carry

        lax.fori_loop(0, (n_items + (RUN - 1)) // RUN, of_run, 0)

    @pl.when(held_at[16] == 0)
    def _():
        def of_item(index, carry):
            block, _ = span_of(items[index])
            cell = block // (ROWS // IB)
            for ox in range(3):
                for oy in range(3):
                    at = ((cell // 8 + ox) * HY + oy) * HZ + cell % 8
                    column = pl.multiple_of(at * SLOTS, SLOTS)
                    multiply(block, [column], form_a, 0)
                    sums = [jnp.zeros((IB, SLOTS), jnp.float32) for _ in range(4)]
                    finish(block, combine(column, form_a, 0, sums))
            return carry

        lax.fori_loop(0, n_items, of_item, 0)

    def of_cell(index, carry):
        turned = acc[pl.ds(pl.multiple_of(index * ROWS, IB), ROWS), :].T[0:8]
        chosen = perm[index]
        moments = jnp.zeros((8, SLOTS), jnp.float32)
        for part in split3(turned):
            moments = moments + jnp.dot(
                part.astype(jnp.bfloat16), chosen, preferred_element_type=jnp.float32
            )
        raw = own[index]
        off = brick_offset(index // 8 + 1, index * 0 + 1, index % 8 + 1)
        occupied = raw[7:8]
        total = [
            noise_scale
            * occupied
            * ((raw[k : k + 1] + off[k]) * moments[3:4] - moments[k : k + 1])
            for k in range(3)
        ]
        state = vf[index]
        v = [state[k : k + 1] for k in range(3)]
        f = [state[k + 3 : k + 4] for k in range(3)]
        new_v = [v[k] + 0.5 * time_step * (f[k] + total[k]) for k in range(3)]
        if mode == "predict":
            out[index] = jnp.concatenate([raw[0:3], *new_v, raw[6:8]], axis=0)
        elif mode == "step":
            moved = [
                raw[k : k + 1] + time_step * new_v[k] + 0.5 * time_step * time_step * total[k]
                for k in range(3)
            ]
            guess = [new_v[k] + predict_weight * time_step * total[k] for k in range(3)]
            out[index] = jnp.concatenate([*moved, *guess, raw[6:8]], axis=0)
            vf_out[index] = jnp.concatenate([*new_v, *total, state[6:8]], axis=0)
        else:
            out[index] = jnp.concatenate([raw[0:3], *new_v, raw[6:8]], axis=0)
            side = state[6:7]
            rows = []
            for h in (0, 1):
                select = jnp.where(side == float(h), occupied, 0.0)
                rows += [new_v[0] * select, new_v[1] * select, new_v[2] * select, select]
            summed = jnp.sum(jnp.concatenate(rows, axis=0), axis=1, keepdims=True)
            lane = lax.broadcasted_iota(jnp.int32, (8, SLOTS), 1)
            bins_out[...] = jnp.where(lane == index, summed, bins_out[...])
        return carry

    if mode == "last":
        bins_out[...] = jnp.zeros_like(bins_out)
    lax.fori_loop(0, 16, of_cell, 0, unroll=2)


def force_call(tag, mode, own, faces, *extra):
    tile = jax.ShapeDtypeStruct((16, 8, SLOTS), jnp.float32)
    shapes = {
        "predict": tile,
        "step": (tile, tile),
        "last": (tile, jax.ShapeDtypeStruct((8, SLOTS), jnp.float32)),
    }[mode]
    vmem = pl.BlockSpec(memory_space=pltpu.VMEM)
    n_out = 1 if mode == "predict" else len(shapes)

    def body(*refs):
        force_kernel(float(tag), mode, *refs)

    return pl.pallas_call(
        body,
        out_shape=shapes,
        in_specs=[vmem] * (5 + len(extra)),
        out_specs=vmem if n_out == 1 else tuple([vmem] * n_out),
        scratch_shapes=[
            pltpu.VMEM((NFEAT, CELLS * SLOTS), jnp.bfloat16),
            pltpu.VMEM((24, CELLS * SLOTS), jnp.float32),
            pltpu.VMEM(((16 * ROWS + IB) * 3, NFEAT), jnp.bfloat16),
            pltpu.VMEM((16, ROWS, SLOTS), jnp.bfloat16),
            pltpu.VMEM((16 * ROWS + IB, SLOTS), jnp.float32),
            pltpu.VMEM((3 * IB, 12 * SLOTS), jnp.float32),
            pltpu.SMEM((ITEMS,), jnp.int32),
            pltpu.SMEM((32,), jnp.int32),
        ],
        cost_estimate=pl.CostEstimate(
            flops=10_000_000, bytes_accessed=1_000_000, transcendentals=0
        ),
        compiler_params=pltpu.CompilerParams(
            vmem_limit_bytes=16 * 2**20
        ),
        name="pair_" + mode,
    )(own, *faces, *extra)


def shifted(block, axis, periodic, up):
    count = lax.axis_size(axis)
    pairs = [(i, i + 1) for i in range(count - 1)]
    if periodic:
        pairs.append((count - 1, 0))
    if not up:
        pairs = [(b, a) for a, b in pairs]
    return lax.ppermute(block, axis, pairs)


def gather_faces(tiles):
    own = tiles.reshape(2, 1, 8, 8, SLOTS)
    ylo = shifted(own, ("gy", "gz"), False, True)
    yhi = shifted(own, ("gy", "gz"), False, False)
    wide = jnp.concatenate([ylo, own, yhi], axis=1)
    xlo = shifted(wide[1:2], "gx", True, True)
    xhi = shifted(wide[0:1], "gx", True, False)
    return tuple(face.reshape(-1, 8, SLOTS) for face in (ylo, yhi, xlo, xhi))


def tail_kernel(group_ref, got, out, full):
    shape = (256, SLOTS)
    lane = lax.broadcasted_iota(jnp.int32, shape, 1)
    row = lax.broadcasted_iota(jnp.int32, shape, 0)
    comp = lane // 32
    at_x, at_z, at_y = (lane // 16) % 2, lane % 16, row % 32

    def lanes(value, shift):
        return pltpu.roll(value, (-shift) % SLOTS, 1)

    def rows(value, shift):
        return pltpu.roll(value, (-shift) % 256, 0)

    def next_x(value):
        swapped = jnp.where(at_x == 0, lanes(value, 16), lanes(value, -16))
        return jnp.where(at_x == 0, swapped, rows(swapped, 32))

    def prev_x(value):
        swapped = jnp.where(at_x == 0, lanes(value, 16), lanes(value, -16))
        return jnp.where(at_x == 1, swapped, rows(swapped, -32))

    def next_y(value):
        return jnp.where(at_y == 31, 0.0, rows(value, 1))

    def prev_y(value):
        return jnp.where(at_y == 0, 0.0, rows(value, -1))

    def next_z(value):
        return jnp.where(at_z == 15, 0.0, lanes(value, 1))

    def prev_z(value):
        return jnp.where(at_z == 0, 0.0, lanes(value, -1))

    def every(value):
        pair = value + lanes(value, 64)
        return pair + lanes(pair, 32)

    def total(value):
        return 0.25 * jnp.sum(jnp.sum(value, axis=0, keepdims=True), axis=1, keepdims=True)

    coupled = got[...]
    change = jnp.where(
        comp == 0,
        next_x(coupled) - prev_x(coupled),
        jnp.where(
            comp == 1,
            next_y(coupled) - prev_y(coupled),
            jnp.where(comp == 2, next_z(coupled) - prev_z(coupled), 0.0),
        ),
    )
    residual = -0.5 * every(change)
    direction = residual
    pressure = jnp.zeros_like(residual)
    norm_now = total(residual * residual)
    for repeat in range(ITERS):
        beside = next_x(direction) + prev_x(direction)
        beside = beside + next_y(direction) + prev_y(direction)
        beside = beside + next_z(direction) + prev_z(direction)
        applied = 6.0 * direction - beside
        step_length = norm_now / total(direction * applied)
        pressure = pressure + step_length * direction
        residual = residual - step_length * applied
        norm_next = total(residual * residual)
        direction = residual + norm_next / norm_now * direction
        norm_now = norm_next
    gradient = jnp.where(
        comp == 0,
        next_x(pressure) - prev_x(pressure),
        jnp.where(
            comp == 1,
            next_y(pressure) - prev_y(pressure),
            next_z(pressure) - prev_z(pressure),
        ),
    )
    full[...] = jnp.where(comp == 3, pressure, coupled - 0.5 * gradient)
    start = pl.multiple_of(group_ref[0] * 8, 8)
    out[...] = full[pl.ds(start, 8), :]


def tail_call(pair_of_groups, got):
    return pl.pallas_call(
        tail_kernel,
        out_shape=jax.ShapeDtypeStruct((8, SLOTS), jnp.float32),
        in_specs=[
            pl.BlockSpec(memory_space=pltpu.SMEM),
            pl.BlockSpec(memory_space=pltpu.VMEM),
        ],
        out_specs=pl.BlockSpec(memory_space=pltpu.VMEM),
        scratch_shapes=[pltpu.VMEM((256, SLOTS), jnp.float32)],
        compiler_params=pltpu.CompilerParams(vmem_limit_bytes=8 * 2**20),
        cost_estimate=pl.CostEstimate(
            flops=10_000_000, bytes_accessed=1_000_000, transcendentals=0
        ),
        name="project",
    )(pair_of_groups, got)


def per_device(
    bead_pos, bead_vel, bead_force, cell_count, pair_seed, bead_half, grid_vel, correlation_map
):
    occupied = (lax.broadcasted_iota(jnp.int32, pair_seed.shape, 3) < cell_count[..., None]).astype(
        jnp.float32
    )
    static = jnp.stack([pair_seed.astype(jnp.float32), bead_half.astype(jnp.float32), occupied])
    beads = jnp.moveaxis(jnp.concatenate([bead_pos, bead_vel, bead_force, static]), 0, -2)
    beads = lax.all_to_all(beads, "gz", 1, 2, tiled=True).reshape(16, 12, SLOTS)
    x, v, f = beads[:, 0:3], beads[:, 3:6], beads[:, 6:9]
    seed, half, occupied = beads[:, 9:10], beads[:, 10:11], beads[:, 11:12]
    position = x + time_step * v + 0.5 * time_step * time_step * f
    guessed = v + predict_weight * time_step * f
    tiles = jnp.concatenate([position, guessed, seed, occupied], axis=1)
    state = jnp.concatenate([v, f, half, occupied], axis=1)

    for step in range(STEPS):
        tag = step + 3
        tiles = force_call(tag, "predict", tiles, gather_faces(tiles), state)
        kind = "step" if step < STEPS - 1 else "last"
        tiles, other = force_call(tag, kind, tiles, gather_faces(tiles), state)
        if kind == "step":
            state = other
        else:
            bins = other
    binned = bins[:, :16].reshape(2, 4, 2, 8).transpose(1, 2, 3, 0).reshape(4, 2, 1, 16)
    flag = correlation_map.astype(jnp.float32)
    mean = binned[:3] / jnp.maximum(binned[3], 1.0)
    coupled = grid_vel + couple_rate * flag * (mean - grid_vel)
    sent = jnp.concatenate([coupled.reshape(1, 96), jnp.zeros((1, 32), jnp.float32)], axis=1)
    got = lax.all_to_all(
        jnp.broadcast_to(sent, (256, SLOTS)), ("gx", "gy", "gz"), 0, 0, tiled=True
    )
    tiles, got = lax.optimization_barrier((tiles, got))
    back = lax.all_to_all(tiles.reshape(2, 1, 8, 8, SLOTS), "gz", 2, 1, tiled=True)
    position = jnp.moveaxis(back[..., 0:3, :], -2, 0)
    velocity = jnp.moveaxis(back[..., 3:6, :], -2, 0)
    ix, iy, iz = (lax.axis_index(a) for a in ("gx", "gy", "gz"))
    group = ix * 8 + iy
    solved = tail_call((group // 2).reshape(1), got)
    mine = lax.dynamic_slice(solved, ((group % 2) * 4, 0), (4, SLOTS))
    owner = lax.dynamic_index_in_dim(mine, iz, 0, keepdims=False).reshape(4, 2, 1, 16)
    brick = lax.dynamic_index_in_dim(mine.reshape(4, 4, 2, 4, 4), iz, 3, keepdims=False)
    brick = brick[:, :3].transpose(1, 2, 0, 3)
    return (position, velocity, owner[:3], owner[3], brick)


def solution(mesh):
    placed = (
        P(None, "gx", "gy", "gz", None),
        P(None, "gx", "gy", "gz", None),
        P(None, "gx", "gy", "gz", None),
        P("gx", "gy", "gz"),
        P("gx", "gy", "gz", None),
        P("gx", "gy", "gz", None),
        P(None, "gx", ("gy", "gz"), None),
        P("gx", ("gy", "gz"), None),
    )
    return jax.shard_map(
        per_device,
        mesh=mesh,
        in_specs=placed,
        out_specs=(
            P(None, "gx", "gy", "gz", None),
            P(None, "gx", "gy", "gz", None),
            P(None, "gx", ("gy", "gz"), None),
            P("gx", ("gy", "gz"), None),
            P(None, "gx", "gy", "gz"),
        ),
        check_vma=False,
    )
```

```python
import math

import jax
import jax.numpy as jnp
from jax import lax
from jax.experimental import pallas as pl
from jax.experimental.pallas import tpu as pltpu
from jax.sharding import PartitionSpec as P

STEPS = 2
ITERS = 4

cell_edge = 3.0
conserve = 25.0
friction = 4.5
noise_scale = 3.0 * math.sqrt(12.0) / math.sqrt(0.04)
time_step = 0.04
predict_weight = 0.65
couple_rate = 0.5
hash_prime = 4093.0

ROUND = 12582912.0
SLOTS = 128
IB = 16
ROWS = 192
NFEAT = 64
HX, HY, HZ = 4, 3, 10
CELLS = HX * HY * HZ
ITEMS = 16 * (ROWS // IB) + 8
RUN = 4
FAR = 1.0e5
damp = -friction / noise_scale
lift = conserve / noise_scale - 0.5 / hash_prime


def rint(value):
    return (value + ROUND) - ROUND


def split3(value):
    hi = value.astype(jnp.bfloat16).astype(jnp.float32)
    rest = value - hi
    mid = rest.astype(jnp.bfloat16).astype(jnp.float32)
    low = (rest - mid).astype(jnp.bfloat16).astype(jnp.float32)
    return hi, mid, low


def rows_of(row, values, default):
    out = default
    for index, value in values:
        out = jnp.where(row == index, value, out)
    return out


def bead_tile(raw, off, row):
    x = raw[0:1] + off[0]
    y = raw[1:2] + off[1]
    z = raw[2:3] + off[2]
    vx = raw[3:4] * damp
    vy = raw[4:5] * damp
    vz = raw[5:6] * damp
    q = x * x + y * y + z * z
    p = x * vx + y * vy + z * vz
    q = jnp.where(raw[7:8] > 0.5, q, FAR)
    return x, y, z, vx, vy, vz, q, p


def centred(seed, tag):
    a = seed + tag
    return jnp.where(a > 2046.0, a - hash_prime, a)


def force_kernel(tag, mode, own, ylo, yhi, xlo, xhi, *rest):
    if mode == "predict":
        vf, out, *scratch = rest
    elif mode == "step":
        vf, out, vf_out, *scratch = rest
    else:
        vf, out, bins_out, *scratch = rest
    feat, posb, left, perm, acc, form_a, items, held_at = scratch
    row8 = lax.broadcasted_iota(jnp.int32, (8, SLOTS), 0)
    row16 = lax.broadcasted_iota(jnp.int32, (16, SLOTS), 0)

    def brick_offset(hx, hy, hz):
        return (
            (hx * 3 - 6).astype(jnp.float32),
            (hy * 3).astype(jnp.float32) - 4.5,
            (hz * 3 - 15).astype(jnp.float32),
        )

    def features(raw, place, bounds):
        hx, hy, hz = place
        tile = jnp.concatenate(bead_tile(raw, brick_offset(hx, hy, hz), row8), axis=0)
        hi, mid, low = split3(tile)
        a = centred(raw[6:7], tag)
        c = rint(a * (1.0 / 64.0))
        d = a - 64.0 * c
        fixed = jnp.where(
            row16 < 3, c, jnp.where(row16 < 6, d, jnp.where(row16 < 9, 1.0, 0.0))
        )
        both = jnp.concatenate([hi, mid, hi, low, hi, mid, fixed], axis=0)
        column = pl.multiple_of(((hx * HY + hy) * HZ + hz) * SLOTS, SLOTS)
        feat[:, pl.ds(column, SLOTS)] = both.astype(jnp.bfloat16)
        posb[:, pl.ds(column, SLOTS)] = jnp.concatenate(
            [jnp.broadcast_to(tile[k : k + 1], (8, SLOTS)) for k in range(3)], axis=0
        )
        there = jnp.where(raw[7:8] > 0.5, raw, 0.5 * cell_edge)
        return (jnp.minimum(bounds[0], there), jnp.maximum(bounds[1], there))

    def of_face(ref, count, place, bounds):
        def body(index, carry):
            return features(ref[index], place(index), carry)

        return lax.fori_loop(0, count, body, bounds, unroll=8)

    def fixed_at(value, like):
        return like * 0 + value

    middle = jnp.full((8, SLOTS), 0.5 * cell_edge, jnp.float32)
    bounds = (middle, middle)
    bounds = of_face(own, 16, lambda i: (i // 8 + 1, fixed_at(1, i), i % 8 + 1), bounds)
    bounds = of_face(ylo, 16, lambda i: (i // 8 + 1, fixed_at(0, i), i % 8 + 1), bounds)
    bounds = of_face(yhi, 16, lambda i: (i // 8 + 1, fixed_at(2, i), i % 8 + 1), bounds)
    bounds = of_face(xlo, 24, lambda i: (fixed_at(0, i), i // 8, i % 8 + 1), bounds)
    bounds = of_face(xhi, 24, lambda i: (fixed_at(3, i), i // 8, i % 8 + 1), bounds)
    nothing = jnp.where(lax.broadcasted_iota(jnp.int32, (NFEAT, SLOTS), 0) == 6, FAR, 0.0)
    nothing = nothing.astype(jnp.bfloat16)
    for column in range(HX * HY):
        for end in (0, HZ - 1):
            at = (column * HZ + end) * SLOTS
            feat[:, at : at + SLOTS] = nothing
            posb[:, at : at + SLOTS] = jnp.zeros((24, SLOTS), jnp.float32)
    least = jnp.min(bounds[0], axis=1, keepdims=True)
    most = jnp.max(bounds[1], axis=1, keepdims=True)
    cut = 0.5 * (least + most)
    span = jnp.maximum(most[0:1] - least[0:1], most[1:2] - least[1:2])
    apart = jnp.where(span < 3.99, 1.0, 0.0)

    before = jnp.where(
        lax.broadcasted_iota(jnp.int32, (SLOTS, SLOTS), 0)
        < lax.broadcasted_iota(jnp.int32, (SLOTS, SLOTS), 1),
        1.0,
        0.0,
    ).astype(jnp.bfloat16)
    place_row = lax.broadcasted_iota(jnp.int32, (ROWS, SLOTS), 0).astype(jnp.float32)

    lane1 = lax.broadcasted_iota(jnp.int32, (1, SLOTS), 1)

    def of_own(index, codes):
        raw = own[index]
        off = brick_offset(index // 8 + 1, index * 0 + 1, index % 8 + 1)
        tile = jnp.concatenate(bead_tile(raw, off, row8), axis=0)
        hi, mid, low = split3(tile)
        a = centred(raw[6:7], tag)
        zero = jnp.zeros((1, SLOTS), jnp.float32)
        one = jnp.ones((1, SLOTS), jnp.float32)

        def s_group(part, last):
            return jnp.concatenate([2.0 * part[0:3], zero, zero, zero, last, zero], axis=0)

        def c_group(part, last):
            return jnp.concatenate([-part[3:6], -part[0:3], zero, last], axis=0)

        x, y, z = tile[0:1], tile[1:2], tile[2:3]
        g3 = split3(1.0 - (x * x + y * y + z * z))
        e3 = split3(tile[7:8])
        a64 = 64.0 * a
        a64 = a64 - hash_prime * rint(a64 * (1.0 / hash_prime))
        b64 = split3(a64 * (1.0 / hash_prime))
        b1 = split3(a * (1.0 / hash_prime))
        shift = split3(jnp.full((1, SLOTS), (0.5 - tag * tag) / hash_prime - 0.5, jnp.float32))
        pad7 = jnp.zeros((7, SLOTS), jnp.float32)
        pad6 = jnp.zeros((6, SLOTS), jnp.float32)
        left_s = jnp.concatenate(
            [
                s_group(hi, -one),
                s_group(hi, -one),
                s_group(mid, zero),
                s_group(hi, -one),
                s_group(low, zero),
                s_group(mid, zero),
                pad6,
                *g3,
                pad7,
            ],
            axis=0,
        )
        left_c = jnp.concatenate(
            [
                c_group(hi, one),
                c_group(hi, one),
                c_group(mid, zero),
                c_group(hi, one),
                c_group(low, zero),
                c_group(mid, zero),
                pad6,
                *e3,
                pad7,
            ],
            axis=0,
        )
        left_u = jnp.concatenate(
            [jnp.zeros((48, SLOTS), jnp.float32), *b64, *b1, *shift, pad7], axis=0
        )
        occupied = jnp.where(raw[7:8] > 0.5, 1.0, 0.0)
        side_x = jnp.where(raw[0:1] > cut[0:1], apart, 0.0)
        side_y = jnp.where(raw[1:2] > cut[1:2], apart, 0.0)
        quarter = 2.0 * side_x + side_y
        masks = jnp.concatenate(
            [jnp.where(quarter == float(g), occupied, 0.0) for g in range(4)]
            + [jnp.zeros((4, SLOTS), jnp.float32)],
            axis=0,
        )
        rank = jnp.dot(masks.astype(jnp.bfloat16), before, preferred_element_type=jnp.float32)
        held = jnp.sum(masks, axis=1, keepdims=True)
        blocks = jnp.floor((held + (IB - 1.0)) * (1.0 / IB))
        first = [jnp.zeros((1, 1), jnp.float32)]
        for g in range(3):
            first.append(first[-1] + blocks[g : g + 1])
        slot = jnp.full((1, SLOTS), -1.0, jnp.float32)
        for g in range(4):
            here = float(IB) * first[g] + rank[g : g + 1]
            slot = jnp.where(masks[g : g + 1] > 0.5, here, slot)
        chosen = jnp.where(place_row == slot, 1.0, 0.0).astype(jnp.bfloat16)
        perm[index] = chosen
        for which, rows in enumerate((left_s, left_c, left_u)):
            turned = rows.T.astype(jnp.bfloat16)
            ordered = jnp.dot(chosen, turned, preferred_element_type=jnp.float32)
            ordered = ordered.astype(jnp.bfloat16)
            for block in range(ROWS // IB):
                start = pl.multiple_of(index * (3 * ROWS) + (block * 3 + which) * IB, IB)
                left[pl.ds(start, IB), :] = ordered[block * IB : (block + 1) * IB]
        code = blocks[0:1] + 16.0 * blocks[1:2] + 256.0 * blocks[2:3] + 4096.0 * blocks[3:4]
        return jnp.where(lane1 == index, code, codes)

    codes = lax.fori_loop(0, 16, of_own, jnp.zeros((1, SLOTS), jnp.float32), unroll=4)
    codes = jnp.where(lane1 == 16, apart, codes).astype(jnp.int32)
    for k in range(17):
        held_at[k] = codes[0, k]

    def list_cell(index, n_items):
        code = held_at[index]
        corner = (index // 8) * (HY * HZ) + index % 8
        row = index * (ROWS // IB) * SLOTS
        for g in range(4):
            first = row + corner + (g // 2) * (HY * HZ) + (g % 2) * HZ

            def put(b, at, first=first):
                items[at] = first + b * SLOTS
                return at + 1

            here = (code >> (4 * g)) & 15
            n_items = lax.fori_loop(0, here, put, n_items)
            row = row + here * SLOTS
        return n_items

    n_items = lax.fori_loop(0, 16, list_cell, jnp.int32(0))
    for extra in range(5):
        items[n_items + extra] = 16 * (ROWS // IB) * SLOTS

    acc[...] = jnp.zeros_like(acc)
    lane16 = lax.broadcasted_iota(jnp.int32, (IB, SLOTS), 1)

    def span_of(item):
        block, cell = item // SLOTS, item % SLOTS
        columns = [cell, cell + HZ, cell + HY * HZ, cell + (HY + 1) * HZ]
        return block, [pl.multiple_of(c * SLOTS, SLOTS) for c in columns]

    wide3 = 3 * SLOTS

    def multiply(block, columns, form, k):
        row = pl.multiple_of(block * (3 * IB), 3 * IB)
        rhs = [feat[:, pl.ds(c, wide3)] for c in columns]
        rhs = rhs[0] if len(rhs) == 1 else jnp.concatenate(rhs, axis=1)
        form[:, k * wide3 : k * wide3 + rhs.shape[1]] = jnp.dot(
            left[pl.ds(row, 3 * IB), :], rhs, preferred_element_type=jnp.float32
        )

    def combine(column, form, k, sums):
        sums = list(sums)
        for piece in range(3):
            lanes = slice((3 * k + piece) * SLOTS, (3 * k + piece + 1) * SLOTS)
            weight = jnp.maximum(form[0:IB, lanes], 0.0)
            u = form[2 * IB : 3 * IB, lanes]
            strength = weight * ((u - rint(u)) + lift + weight * form[IB : 2 * IB, lanes])
            here = posb[:, pl.ds(pl.multiple_of(column + piece * SLOTS, SLOTS), SLOTS)]
            for d in range(3):
                wide = jnp.concatenate([here[8 * d : 8 * d + 8]] * (IB // 8), axis=0)
                sums[d] = sums[d] + strength * wide
            sums[3] = sums[3] + strength
        return sums

    def finish(block, sums):
        gathered = jnp.zeros((IB, SLOTS), jnp.float32)
        for d in range(4):
            whole = jnp.sum(sums[d], axis=1, keepdims=True)
            gathered = jnp.where(lane16 == d, whole, gathered)
        row = pl.multiple_of(block * IB, IB)
        acc[pl.ds(row, IB), :] = acc[pl.ds(row, IB), :] + gathered

    @pl.when(held_at[16] == 1)
    def _():
        block, columns = span_of(items[0])
        for k in (0, 2):
            multiply(block, columns[k : k + 2], form_a, k)

        def of_run(index, carry):
            spans = [span_of(items[RUN * index + k]) for k in range(RUN + 1)]
            for turn in range(RUN):
                block, columns = spans[turn]
                later_block, later_columns = spans[turn + 1]
                sums = [jnp.zeros((IB, SLOTS), jnp.float32) for _ in range(4)]
                for k in (0, 2):
                    sums = combine(columns[k], form_a, k, sums)
                    sums = combine(columns[k + 1], form_a, k + 1, sums)
                    multiply(later_block, later_columns[k : k + 2], form_a, k)
                finish(block, sums)
            return carry

        lax.fori_loop(0, (n_items + (RUN - 1)) // RUN, of_run, 0)

    @pl.when(held_at[16] == 0)
    def _():
        def of_item(index, carry):
            block, _ = span_of(items[index])
            cell = block // (ROWS // IB)
            for ox in range(3):
                for oy in range(3):
                    at = ((cell // 8 + ox) * HY + oy) * HZ + cell % 8
                    column = pl.multiple_of(at * SLOTS, SLOTS)
                    multiply(block, [column], form_a, 0)
                    sums = [jnp.zeros((IB, SLOTS), jnp.float32) for _ in range(4)]
                    finish(block, combine(column, form_a, 0, sums))
            return carry

        lax.fori_loop(0, n_items, of_item, 0)

    def of_cell(index, carry):
        turned = acc[pl.ds(pl.multiple_of(index * ROWS, IB), ROWS), :].T[0:8]
        chosen = perm[index]
        moments = jnp.zeros((8, SLOTS), jnp.float32)
        for part in split3(turned):
            moments = moments + jnp.dot(
                part.astype(jnp.bfloat16), chosen, preferred_element_type=jnp.float32
            )
        raw = own[index]
        off = brick_offset(index // 8 + 1, index * 0 + 1, index % 8 + 1)
        occupied = raw[7:8]
        total = [
            noise_scale
            * occupied
            * ((raw[k : k + 1] + off[k]) * moments[3:4] - moments[k : k + 1])
            for k in range(3)
        ]
        state = vf[index]
        v = [state[k : k + 1] for k in range(3)]
        f = [state[k + 3 : k + 4] for k in range(3)]
        new_v = [v[k] + 0.5 * time_step * (f[k] + total[k]) for k in range(3)]
        if mode == "predict":
            out[index] = jnp.concatenate([raw[0:3], *new_v, raw[6:8]], axis=0)
        elif mode == "step":
            moved = [
                raw[k : k + 1] + time_step * new_v[k] + 0.5 * time_step * time_step * total[k]
                for k in range(3)
            ]
            guess = [new_v[k] + predict_weight * time_step * total[k] for k in range(3)]
            out[index] = jnp.concatenate([*moved, *guess, raw[6:8]], axis=0)
            vf_out[index] = jnp.concatenate([*new_v, *total, state[6:8]], axis=0)
        else:
            out[index] = jnp.concatenate([raw[0:3], *new_v, raw[6:8]], axis=0)
            side = state[6:7]
            rows = []
            for h in (0, 1):
                select = jnp.where(side == float(h), occupied, 0.0)
                rows += [new_v[0] * select, new_v[1] * select, new_v[2] * select, select]
            summed = jnp.sum(jnp.concatenate(rows, axis=0), axis=1, keepdims=True)
            lane = lax.broadcasted_iota(jnp.int32, (8, SLOTS), 1)
            bins_out[...] = jnp.where(lane == index, summed, bins_out[...])
        return carry

    if mode == "last":
        bins_out[...] = jnp.zeros_like(bins_out)
    lax.fori_loop(0, 16, of_cell, 0, unroll=4)


def force_call(tag, mode, own, faces, *extra):
    tile = jax.ShapeDtypeStruct((16, 8, SLOTS), jnp.float32)
    shapes = {
        "predict": tile,
        "step": (tile, tile),
        "last": (tile, jax.ShapeDtypeStruct((8, SLOTS), jnp.float32)),
    }[mode]
    vmem = pl.BlockSpec(memory_space=pltpu.VMEM)
    n_out = 1 if mode == "predict" else len(shapes)

    def body(*refs):
        force_kernel(float(tag), mode, *refs)

    return pl.pallas_call(
        body,
        out_shape=shapes,
        in_specs=[vmem] * (5 + len(extra)),
        out_specs=vmem if n_out == 1 else tuple([vmem] * n_out),
        scratch_shapes=[
            pltpu.VMEM((NFEAT, CELLS * SLOTS), jnp.bfloat16),
            pltpu.VMEM((24, CELLS * SLOTS), jnp.float32),
            pltpu.VMEM(((16 * ROWS + IB) * 3, NFEAT), jnp.bfloat16),
            pltpu.VMEM((16, ROWS, SLOTS), jnp.bfloat16),
            pltpu.VMEM((16 * ROWS + IB, SLOTS), jnp.float32),
            pltpu.VMEM((3 * IB, 12 * SLOTS), jnp.float32),
            pltpu.SMEM((ITEMS,), jnp.int32),
            pltpu.SMEM((32,), jnp.int32),
        ],
        cost_estimate=pl.CostEstimate(
            flops=10_000_000, bytes_accessed=1_000_000, transcendentals=0
        ),
        compiler_params=pltpu.CompilerParams(
            vmem_limit_bytes=16 * 2**20
        ),
        name="pair_" + mode,
    )(own, *faces, *extra)


def shifted(block, axis, periodic, up):
    count = lax.axis_size(axis)
    pairs = [(i, i + 1) for i in range(count - 1)]
    if periodic:
        pairs.append((count - 1, 0))
    if not up:
        pairs = [(b, a) for a, b in pairs]
    return lax.ppermute(block, axis, pairs)


def gather_faces(tiles):
    own = tiles.reshape(2, 1, 8, 8, SLOTS)
    ylo = shifted(own, ("gy", "gz"), False, True)
    yhi = shifted(own, ("gy", "gz"), False, False)
    wide = jnp.concatenate([ylo, own, yhi], axis=1)
    xlo = shifted(wide[1:2], "gx", True, True)
    xhi = shifted(wide[0:1], "gx", True, False)
    return tuple(face.reshape(-1, 8, SLOTS) for face in (ylo, yhi, xlo, xhi))


def tail_kernel(group_ref, got, out, full):
    shape = (256, SLOTS)
    lane = lax.broadcasted_iota(jnp.int32, shape, 1)
    row = lax.broadcasted_iota(jnp.int32, shape, 0)
    comp = lane // 32
    at_x, at_z, at_y = (lane // 16) % 2, lane % 16, row % 32

    def lanes(value, shift):
        return pltpu.roll(value, (-shift) % SLOTS, 1)

    def rows(value, shift):
        return pltpu.roll(value, (-shift) % 256, 0)

    def next_x(value):
        swapped = jnp.where(at_x == 0, lanes(value, 16), lanes(value, -16))
        return jnp.where(at_x == 0, swapped, rows(swapped, 32))

    def prev_x(value):
        swapped = jnp.where(at_x == 0, lanes(value, 16), lanes(value, -16))
        return jnp.where(at_x == 1, swapped, rows(swapped, -32))

    def next_y(value):
        return jnp.where(at_y == 31, 0.0, rows(value, 1))

    def prev_y(value):
        return jnp.where(at_y == 0, 0.0, rows(value, -1))

    def next_z(value):
        return jnp.where(at_z == 15, 0.0, lanes(value, 1))

    def prev_z(value):
        return jnp.where(at_z == 0, 0.0, lanes(value, -1))

    def every(value):
        pair = value + lanes(value, 64)
        return pair + lanes(pair, 32)

    def total(value):
        return 0.25 * jnp.sum(jnp.sum(value, axis=0, keepdims=True), axis=1, keepdims=True)

    coupled = got[...]
    change = jnp.where(
        comp == 0,
        next_x(coupled) - prev_x(coupled),
        jnp.where(
            comp == 1,
            next_y(coupled) - prev_y(coupled),
            jnp.where(comp == 2, next_z(coupled) - prev_z(coupled), 0.0),
        ),
    )
    residual = -0.5 * every(change)
    direction = residual
    pressure = jnp.zeros_like(residual)
    norm_now = total(residual * residual)
    for repeat in range(ITERS):
        beside = next_x(direction) + prev_x(direction)
        beside = beside + next_y(direction) + prev_y(direction)
        beside = beside + next_z(direction) + prev_z(direction)
        applied = 6.0 * direction - beside
        step_length = norm_now / total(direction * applied)
        pressure = pressure + step_length * direction
        residual = residual - step_length * applied
        norm_next = total(residual * residual)
        direction = residual + norm_next / norm_now * direction
        norm_now = norm_next
    gradient = jnp.where(
        comp == 0,
        next_x(pressure) - prev_x(pressure),
        jnp.where(
            comp == 1,
            next_y(pressure) - prev_y(pressure),
            next_z(pressure) - prev_z(pressure),
        ),
    )
    full[...] = jnp.where(comp == 3, pressure, coupled - 0.5 * gradient)
    start = pl.multiple_of(group_ref[0] * 8, 8)
    out[...] = full[pl.ds(start, 8), :]


def tail_call(pair_of_groups, got):
    return pl.pallas_call(
        tail_kernel,
        out_shape=jax.ShapeDtypeStruct((8, SLOTS), jnp.float32),
        in_specs=[
            pl.BlockSpec(memory_space=pltpu.SMEM),
            pl.BlockSpec(memory_space=pltpu.VMEM),
        ],
        out_specs=pl.BlockSpec(memory_space=pltpu.VMEM),
        scratch_shapes=[pltpu.VMEM((256, SLOTS), jnp.float32)],
        compiler_params=pltpu.CompilerParams(vmem_limit_bytes=8 * 2**20),
        cost_estimate=pl.CostEstimate(
            flops=10_000_000, bytes_accessed=1_000_000, transcendentals=0
        ),
        name="project",
    )(pair_of_groups, got)


def per_device(
    bead_pos, bead_vel, bead_force, cell_count, pair_seed, bead_half, grid_vel, correlation_map
):
    occupied = (lax.broadcasted_iota(jnp.int32, pair_seed.shape, 3) < cell_count[..., None]).astype(
        jnp.float32
    )
    static = jnp.stack([pair_seed.astype(jnp.float32), bead_half.astype(jnp.float32), occupied])
    beads = jnp.moveaxis(jnp.concatenate([bead_pos, bead_vel, bead_force, static]), 0, -2)
    beads = lax.all_to_all(beads, "gz", 1, 2, tiled=True).reshape(16, 12, SLOTS)
    x, v, f = beads[:, 0:3], beads[:, 3:6], beads[:, 6:9]
    seed, half, occupied = beads[:, 9:10], beads[:, 10:11], beads[:, 11:12]
    position = x + time_step * v + 0.5 * time_step * time_step * f
    guessed = v + predict_weight * time_step * f
    tiles = jnp.concatenate([position, guessed, seed, occupied], axis=1)
    state = jnp.concatenate([v, f, half, occupied], axis=1)

    for step in range(STEPS):
        tag = step + 3
        tiles = force_call(tag, "predict", tiles, gather_faces(tiles), state)
        kind = "step" if step < STEPS - 1 else "last"
        tiles, other = force_call(tag, kind, tiles, gather_faces(tiles), state)
        if kind == "step":
            state = other
        else:
            bins = other
    binned = bins[:, :16].reshape(2, 4, 2, 8).transpose(1, 2, 3, 0).reshape(4, 2, 1, 16)
    flag = correlation_map.astype(jnp.float32)
    mean = binned[:3] / jnp.maximum(binned[3], 1.0)
    coupled = grid_vel + couple_rate * flag * (mean - grid_vel)
    sent = jnp.concatenate([coupled.reshape(1, 96), jnp.zeros((1, 32), jnp.float32)], axis=1)
    got = lax.all_to_all(
        jnp.broadcast_to(sent, (256, SLOTS)), ("gx", "gy", "gz"), 0, 0, tiled=True
    )
    tiles, got = lax.optimization_barrier((tiles, got))
    back = lax.all_to_all(tiles.reshape(2, 1, 8, 8, SLOTS), "gz", 2, 1, tiled=True)
    position = jnp.moveaxis(back[..., 0:3, :], -2, 0)
    velocity = jnp.moveaxis(back[..., 3:6, :], -2, 0)
    ix, iy, iz = (lax.axis_index(a) for a in ("gx", "gy", "gz"))
    group = ix * 8 + iy
    solved = tail_call((group // 2).reshape(1), got)
    mine = lax.dynamic_slice(solved, ((group % 2) * 4, 0), (4, SLOTS))
    owner = lax.dynamic_index_in_dim(mine, iz, 0, keepdims=False).reshape(4, 2, 1, 16)
    brick = lax.dynamic_index_in_dim(mine.reshape(4, 4, 2, 4, 4), iz, 3, keepdims=False)
    brick = brick[:, :3].transpose(1, 2, 0, 3)
    return (position, velocity, owner[:3], owner[3], brick)


def solution(mesh):
    placed = (
        P(None, "gx", "gy", "gz", None),
        P(None, "gx", "gy", "gz", None),
        P(None, "gx", "gy", "gz", None),
        P("gx", "gy", "gz"),
        P("gx", "gy", "gz", None),
        P("gx", "gy", "gz", None),
        P(None, "gx", ("gy", "gz"), None),
        P("gx", ("gy", "gz"), None),
    )
    return jax.shard_map(
        per_device,
        mesh=mesh,
        in_specs=placed,
        out_specs=(
            P(None, "gx", "gy", "gz", None),
            P(None, "gx", "gy", "gz", None),
            P(None, "gx", ("gy", "gz"), None),
            P("gx", ("gy", "gz"), None),
            P(None, "gx", "gy", "gz"),
        ),
        check_vma=False,
    )
```
